1024 devices in a mesh: dp: 16 (over y, core), expert: 64 (over z, x).
Axes of the slice: x: 4, y: 8, z: 16, core: 2. Of those that a mesh axis runs over, the one named last changes fastest.
Arguments:
- tokens: bfloat16 [4096, 7168], P('expert', 'dp'), may hold values from -6 to 6
- expert_ids: int32 [4096, 8], P('expert'), may hold values from 0 to 63, all different within a row; in each aligned block of 64 rows (0 to 63, 64 to 127, ...) at most 10 rows name the same one
- combine_weights: float32 [4096, 8], P('expert'), may hold values from 0.05 to 0.6
- w_gate: bfloat16 [64, 7168, 1024], P('expert', 'dp'), may hold values from -0.0625 to 0.0625
- w_up: bfloat16 [64, 7168, 1024], P('expert', 'dp'), may hold values from -0.0625 to 0.0625
- w_down: bfloat16 [64, 1024, 7168], P('expert', None, 'dp'), may hold values from -0.1875 to 0.1875
Outputs:
- combined: bfloat16 [4096, 7168], P('expert', 'dp')
The draws below stay inside these ranges and needn't reach their ends.
Inputs may be any that keep to these rules, and one draw needn't show every extreme that they name: `expert_ids`: each row names 8 different experts. Within the rows of one device (aligned blocks of 64 rows) no expert is named by more than 10 rows, a bound that some block reaches.
All inputs are finite; a program needn't handle non-finite values.
Results may differ from the reference program's by a relative error of at most 0.0057.
Values may be sent and summed in bfloat16 or wider, within the bound.
A program may use at most 64 MiB of HBM per device.

```python
import math
import jax
import jax.numpy as jnp
import numpy as np
from jax import lax

D = 7168
TOP = 8
FF = 1024
EXPERTS = 64
TOK_DEV = 64
TOKENS = 4096
CAP = 10
N_EXPERT = 64


def levels(stream_key, dims, pieces, smallest, largest):
    def one(dim, parts):
        draws = jax.random.uniform(jax.random.fold_in(jax.random.fold_in(stream_key, 6), dim), (parts,), jnp.float32, smallest / len(pieces), largest / len(pieces))
        return jnp.repeat(jnp.exp(draws), dims[dim] // parts).reshape((-1,) + (1,) * (len(dims) - dim - 1))

    level = one(*pieces[0])
    for cut in pieces[1:]:
        level = level * one(*cut)
    return level


def routed_block(stream_key, own, number, rows, amount, top, bound, slope):
    order = jax.random.permutation(stream_key, amount)
    crowded, common = shares(amount, rows * top, bound, slope, True), shares(amount, rows * top, bound, slope, False)
    places = jnp.arange(amount)

    def named(lengths, turn):
        used = int((lengths > 0).sum())
        fixed = max(1, used // 4)
        passed = fixed + (places - fixed + turn * (used - fixed)) % max(1, amount - fixed)
        return jnp.zeros((amount,), jnp.int32).at[order[jnp.where(places < fixed, places, passed)]].set(jnp.asarray(lengths, jnp.int32))

    lengths = jnp.where(number % 4 == 0, named(crowded, number // 4), named(common, number - number // 4 - 1))
    mixed = jax.random.permutation(jax.random.fold_in(own, 3), amount)
    donor, sink = mixed[0:amount // 2 * 2:2], mixed[1:amount // 2 * 2:2]
    room = jnp.minimum(lengths[donor] - 1, bound - lengths[sink]) // 2
    room = jnp.where((donor == order[0]) | (sink == order[0]) | (lengths[sink] == 0), 0, jnp.maximum(room, 0))
    passed = jax.random.randint(jax.random.fold_in(own, 4), (amount // 2,), 0, 1 << 20) % (room + 1)
    lengths = lengths.at[donor].add(-passed).at[sink].add(passed)
    items = jnp.searchsorted(jnp.cumsum(lengths), jnp.arange(rows * top), side="right").astype(jnp.int32)
    listing = items.reshape(top, rows).T
    listing = listing[jax.random.permutation(jax.random.fold_in(own, 1), rows)]
    turn = jax.random.randint(jax.random.fold_in(own, 2), (rows, 1), 0, top)
    return jnp.take_along_axis(listing, (jnp.arange(top)[None, :] + turn) % top, axis=1)


def shares(number_of, total, most, slope, full):
    loads = [(1 << 20) // math.isqrt(grade ** slope) + 1 for grade in range(1, number_of + 1)]
    largest = most if full else min(most, max(-(-total // number_of), total * loads[0] // sum(loads)))
    least = 1 if total - largest >= number_of - 1 else 0
    counts, spare = [largest] + [least] * (number_of - 1), total - largest - least * (number_of - 1)
    while spare > 0:
        free = [i for i in range(1, number_of) if counts[i] < largest] or [i for i in range(1, number_of) if counts[i] < most]
        whole, budget = sum([loads[i] for i in free]), spare
        for i in free:
            addition = min(most - counts[i], max(1, budget * loads[i] // whole), spare)
            counts[i] = counts[i] + addition
            spare = spare - addition
    return np.array(counts)


def normal_values(stream_key, shape, scale, most, cuts=(), held_as=jnp.bfloat16):
    entries = scale * jax.random.normal(stream_key, shape, jnp.float32)
    if cuts:
        entries = entries * levels(stream_key, shape, cuts, -0.22, 0.18)
    return jnp.clip(entries, -most, most).astype(held_as)


def setup_inputs(seed: int = 0) -> dict:
    key_of = jax.random.split(jax.random.key(seed), 7)
    tokens = normal_values(key_of[0], (TOKENS, D), 1.0, 6.0, ((0, 64), (1, 16)))
    expert_ids_keys = jax.random.split(jax.random.fold_in(key_of[1], 1), TOKENS // TOK_DEV)
    expert_ids_turns = jax.random.permutation(jax.random.fold_in(key_of[1], 3), TOKENS // TOK_DEV)
    expert_ids = jax.vmap(lambda own, number: routed_block(jax.random.fold_in(key_of[1], 2), own, number, TOK_DEV, EXPERTS, TOP, CAP, 2))(expert_ids_keys, expert_ids_turns).reshape((TOKENS, TOP))
    combine_weights = jnp.clip(jnp.exp(math.log(0.6) - 2.4849067 * jax.random.uniform(key_of[2], (TOKENS, TOP), jnp.float32) ** levels(key_of[2], (TOKENS, TOP), ((0, 64),), -0.2, 0.2)), 0.05, 0.6)
    w_gate = normal_values(key_of[3], (EXPERTS, D, FF), D ** -0.5, 0.0625, ((0, 64), (1, 16)))
    w_up = normal_values(key_of[4], (EXPERTS, D, FF), D ** -0.5, 0.0625, ((0, 64), (1, 16)))
    w_down = normal_values(key_of[5], (EXPERTS, FF, D), FF ** -0.5, 0.1875, ((0, 64), (2, 16)))
    return {"tokens": tokens, "expert_ids": expert_ids, "combine_weights": combine_weights, "w_gate": w_gate, "w_up": w_up, "w_down": w_down}


def reference(tokens, expert_ids, combine_weights, w_gate, w_up, w_down):
    limit = N_EXPERT * CAP

    def one_expert(total, item):
        number, gate_w, up_w, down_w = item
        matches = expert_ids == number
        chosen = jnp.any(matches, axis=1)
        weight_row = jnp.sum(jnp.where(matches, combine_weights, jnp.zeros_like(combine_weights)), axis=1)
        picked = jnp.nonzero(chosen, size=limit, fill_value=0)[0].astype(jnp.int32)
        valid = (jnp.arange(limit, dtype=jnp.int32) < jnp.sum(chosen.astype(jnp.int32))).astype(jnp.float32)
        arrived = tokens[picked]
        gate_sum = jnp.dot(arrived, gate_w, preferred_element_type=jnp.float32)
        up_sum = jnp.dot(arrived, up_w, preferred_element_type=jnp.float32)
        hidden = (jax.nn.silu(gate_sum) * up_sum).astype(jnp.bfloat16)
        expert_out = jnp.dot(hidden, down_w, preferred_element_type=jnp.float32).astype(jnp.bfloat16)
        scaled = (weight_row[picked] * valid)[:, None] * expert_out.astype(jnp.float32)
        return total.at[picked].add(scaled), None

    start = jnp.zeros((TOKENS, D), jnp.float32)
    numbers = jnp.arange(EXPERTS, dtype=jnp.int32)
    total, unused = lax.scan(one_expert, start, (numbers, w_gate, w_up, w_down))
    return total.astype(jnp.bfloat16)
```

```python
import jax
import jax.numpy as jnp
from jax import lax
from jax.experimental import pallas as pl
from jax.experimental.pallas import tpu as pltpu
from jax.sharding import PartitionSpec as P

CAP = 10
NZ, NX, NY = 16, 4, 8
MESH = pl.DeviceIdType.MESH
F32, BF16 = jnp.float32, jnp.bfloat16


def place(sigma):
    return (sigma + 3) % NZ


def body(
    tok, ids, wts, wg_hbm, wu_hbm, wd_hbm, out,
    wg, wu, wd, blk, meta, xs, xr, wt_hi, wt_lo, part, prx, sb, rr, hid, ob, yb, pt, zs, rz,
    w_sem, own_sem, za_s, za_r, zm_s, zm_r, xa_s, xa_r, pp_s, pp_r, rs_s, rs_r,
    ag_s, ag_r, ph_s, ph_r, xb_s, xb_r, zr_s, zr_r,
):
    width = tok.shape[1]
    d, e = lax.axis_index("dp"), lax.axis_index("expert")
    y, c = d // 2, d % 2
    z, x = e // NX, e % NX

    z_dev = ({"expert": ((z + 1) % NZ) * NX + x}, {"expert": ((z + NZ - 1) % NZ) * NX + x})
    x_fwd = [None] + [{"expert": z * NX + (x + j) % NX} for j in range(1, NX)]
    x_bwd = [None] + [{"expert": z * NX + (x + NX - j) % NX} for j in range(1, NX)]
    y_dev = ({"dp": ((y + 1) % NY) * 2 + c}, {"dp": ((y + NY - 1) % NY) * 2 + c})
    partner = {"dp": y * 2 + (1 - c)}

    def remote(src, dst, ssem, rsem, dev):
        return pltpu.make_async_remote_copy(
            src_ref=src, dst_ref=dst, send_sem=ssem, recv_sem=rsem, device_id=dev, device_id_type=MESH
        )

    loads = [
        pltpu.make_async_copy(wg_hbm.at[0], wg, w_sem.at[0]),
        pltpu.make_async_copy(wu_hbm.at[0], wu, w_sem.at[1]),
        pltpu.make_async_copy(wd_hbm.at[0], wd, w_sem.at[2]),
    ]
    for load in loads:
        load.start()
    keep = pltpu.make_async_copy(tok, blk.at[place(0)], own_sem)
    keep.start()

    barrier = pltpu.get_barrier_semaphore()
    for dev in (*z_dev, *x_fwd[1:], *y_dev, partner):
        pl.semaphore_signal(barrier, inc=1, device_id=dev, device_id_type=MESH)

    e_iota = lax.broadcasted_iota(jnp.int32, (64, 64), 0)
    t_iota = lax.broadcasted_iota(jnp.int32, (64, 64), 1)
    named = jnp.zeros((64, 64), F32)
    for k in range(8):
        named = named + (e_iota == ids[k : k + 1, :]).astype(F32)
    before = jnp.dot(
        named.astype(BF16), (e_iota < t_iota).astype(F32).astype(BF16), preferred_element_type=F32
    )
    for k in range(8):
        row = ids[k : k + 1, :]
        position = jnp.sum(jnp.where(e_iota == row, before, 0.0), axis=0, keepdims=True)
        meta[place(0), k : k + 1, 0:64] = row.astype(F32) * 16.0 + position
    meta[place(0), :, 64:128] = wts[...]

    pl.semaphore_wait(barrier, 8)

    def ring_place(way, k):
        return place(k if way == 0 else (NZ - k) % NZ)

    half = 32
    za, zm = {}, {}
    for way in range(2):
        for k in range(1, 9):
            for sub in range(2):
                if k == 8 and sub != way:
                    continue
                rows = pl.ds(sub * half, half)
                src = tok.at[rows] if k == 1 else blk.at[ring_place(way, k - 1), rows]
                za[way, k, sub] = remote(
                    src, blk.at[ring_place(way, k), rows], za_s.at[way, k - 1, sub], za_r.at[way, k - 1, sub], z_dev[way]
                )
            if k < 8 or way == 0:
                zm[way, k] = remote(
                    meta.at[ring_place(way, k - 1)], meta.at[ring_place(way, k)],
                    zm_s.at[way, k - 1], zm_r.at[way, k - 1], z_dev[way],
                )

    def z_step(k):
        for sub in range(2):
            for way in range(2):
                if sub == 0:
                    if k > 1:
                        zm[way, k - 1].wait_recv()
                    if (way, k) in zm:
                        zm[way, k].start()
                if k > 1:
                    za[way, k - 1, sub].wait_recv()
                if (way, k, sub) in za:
                    za[way, k, sub].start()

    lane = lax.broadcasted_iota(jnp.int32, (8, 128), 1)
    row_iota = lax.broadcasted_iota(jnp.int32, (80, 512), 0).astype(F32)
    src_row = (lax.broadcasted_iota(jnp.int32, (1, 512), 1) // 64 * CAP).astype(F32)
    xa = {}
    for g in range(2):
        for j in range(1, NX):
            xa[g, j] = remote(xs.at[g, j - 1], xr.at[g, j], xa_s.at[g, j - 1], xa_r.at[g, j - 1], x_fwd[j])

    def select(g):
        codes, weights = [], []
        for s in range(0, 8, 2):
            a, b = meta[8 * g + s], meta[8 * g + s + 1]
            codes.append(jnp.where(lane < 64, a, pltpu.roll(b, 64, 1)))
            weights.append(jnp.where(lane < 64, pltpu.roll(a, 64, 1), b))
        code = jnp.concatenate(codes, axis=1)
        weight = jnp.concatenate(weights, axis=1)
        rows = blk[8 * g : 8 * g + 8].reshape(512, width)
        for j in (2, 1, 3, 0):
            base = ((z * NX + (x + j) % NX) * 16).astype(F32)
            own = code - base
            hit = jnp.logical_and(own >= 0.0, own < 16.0)
            slot = jnp.max(jnp.where(hit, own, -1.0), axis=0, keepdims=True)
            share = jnp.sum(jnp.where(hit, weight, 0.0), axis=0, keepdims=True)
            target = jnp.where(slot >= 0.0, slot + src_row, -1.0)
            chosen = row_iota == target
            pick = jnp.dot(chosen.astype(F32).astype(BF16), rows, preferred_element_type=F32).astype(BF16)
            if j:
                xs[g, j - 1] = pick
                xa[g, j].start()
            else:
                xr[g, 0] = pick
            scaled = jnp.where(chosen, share, 0.0)
            high = scaled.astype(BF16)
            wt_hi[g, 80 * j : 80 * j + 80, :] = high
            wt_lo[g, 80 * j : 80 * j + 80, :] = (scaled - high.astype(F32)).astype(BF16)

    def pair(g, s):
        return remote(part.at[g, s, 1 - c], prx.at[g, s], pp_s.at[g, s], pp_r.at[g, s], partner)

    def parts(g):
        rows = xr[g].reshape(320, width)

        def piece(s, carry):
            at_g = pl.multiple_of((y + 2 * NY - 1 - s) % NY * 128, 128)
            at_u = pl.multiple_of((y + 1 + s) % NY * 128, 128)
            gate = jnp.dot(rows, wg[:, pl.ds(at_g, 128)], preferred_element_type=F32)
            up = jnp.dot(rows, wu[:, pl.ds(at_u, 128)], preferred_element_type=F32)
            part[g, s, :, 0] = gate.reshape(2, 160, 128)
            part[g, s, :, 1] = up.reshape(2, 160, 128)
            pair(g, s).start()
            return carry

        lax.fori_loop(0, NY, piece, 0)

    rs = {}
    for g in range(2):
        for s in range(NY - 1):
            for m in range(2):
                rs[g, s, m] = remote(sb.at[g, s, m], rr.at[g, s, m], rs_s.at[g, s, m], rs_r.at[g, s, m], y_dev[m])

    def y_step(g, s):
        pair(g, s).wait_recv()
        for m in range(2):
            value = part[g, s, c, m] + prx[g, s, m]
            if s:
                rs[g, s - 1, m].wait_recv()
                value = value + rr[g, s - 1, m]
            sb[g, s, m] = value
            rs[g, s, m].start()

    def unit(k):
        return pl.ds(pl.multiple_of((y + 2 * NY - k) % NY * 128, 128), 128)

    ag, ph = {}, {}
    for g in range(2):
        for way in range(2):
            last = 4 if way == g else 3
            for k in range(1, last + 1):
                near = unit(k - 1 if way == 0 else 1 - k)
                there = hid.at[g, c, :, near]
                ag[g, way, k] = remote(there, there, ag_s.at[g, way, k - 1], ag_r.at[g, way, k - 1], y_dev[way])
        for sigma in range(-4, 5):
            ph[g, sigma] = None

    def hand(g, index, sigma):
        there = hid.at[g, c, :, unit(sigma)]
        return remote(there, hid.at[g, c, :, unit(sigma)], ph_s.at[g, index], ph_r.at[g, index], partner)

    def received(g, index, sigma):
        there = hid.at[g, 1 - c, :, unit(sigma)]
        return remote(there, there, ph_s.at[g, index], ph_r.at[g, index], partner)

    def arrived(g, way, k):
        there = hid.at[g, c, :, unit(k if way == 0 else -k)]
        return remote(there, there, ag_s.at[g, way, k - 1], ag_r.at[g, way, k - 1], y_dev[way])

    def activate(g):
        pair(g, NY - 1).wait_recv()
        for m in range(2):
            rs[g, NY - 2, m].wait_recv()
        gate = part[g, NY - 1, c, 0] + prx[g, NY - 1, 0] + rr[g, NY - 2, 0]
        up = part[g, NY - 1, c, 1] + prx[g, NY - 1, 1] + rr[g, NY - 2, 1]
        hid[g, c, :, unit(0)] = (gate / (1.0 + jnp.exp(-gate)) * up).astype(BF16)
        for way in range(2):
            ag[g, way, 1].start()
        hand(g, 0, 0).start()

    order = {g: [0] for g in range(2)}

    def gather_step(g, k):
        for way in range(2):
            if (g, way, k) not in ag:
                continue
            arrived(g, way, k).wait_recv()
            if (g, way, k + 1) in ag:
                ag[g, way, k + 1].start()
            sigma = k if way == 0 else -k
            hand(g, len(order[g]), sigma).start()
            order[g].append(sigma)

    xb = {}
    for g in range(2):
        for j in range(1, NX):
            xb[g, j] = remote(ob.at[g, j], yb.at[g, j], xb_s.at[g, j - 1], xb_r.at[g, j - 1], x_bwd[j])

    def down(g):
        for index, sigma in enumerate(order[g]):
            received(g, index, sigma).wait_recv()
        for h in (1, 0):
            res = jnp.dot(hid[g, h], wd[...], preferred_element_type=F32).astype(BF16).reshape(2, 80, width)
            if h:
                ob[g, 2] = res[0]
                xb[g, 2].start()
                ob[g, 3] = res[1]
                xb[g, 3].start()
            else:
                ob[g, 1] = res[1]
                xb[g, 1].start()
                yb[g, 0] = res[0]

    def combine(g):
        for j in range(1, NX):
            xb[g, j].wait_recv()
        rows = yb[g].reshape(320, width)
        dims = (((0,), (0,)), ((), ()))
        res = lax.dot_general(wt_hi[g], rows, dims, preferred_element_type=F32)
        res = res + lax.dot_general(wt_lo[g], rows, dims, preferred_element_type=F32)
        pt[8 * g : 8 * g + 8] = res.reshape(8, 64, width)

    zr = {}
    for way in range(2):
        for k in range(1, 9):
            for sub in range(2):
                if k == 8 and sub != way:
                    continue
                zr[way, k, sub] = remote(
                    zs.at[way, k - 1, sub], rz.at[way, k - 1, sub], zr_s.at[way, k - 1, sub], zr_r.at[way, k - 1, sub], z_dev[way]
                )

    def z_sum(k):
        for sub in range(2):
            for way in range(2):
                if (way, k, sub) not in zr:
                    continue
                at = ring_place(1 - way, k)
                value = pt[at, sub * half : (sub + 1) * half, :]
                if (way, k + 1, sub) in zr:
                    zr[way, k + 1, sub].wait_recv()
                    value = value + rz[way, k, sub].astype(F32)
                zs[way, k - 1, sub] = value.astype(BF16)
                zr[way, k, sub].start()

    for k in range(1, 6):
        z_step(k)
    keep.wait()
    select(0)
    for k in range(6, 9):
        z_step(k)
    za[0, 8, 0].wait_recv()
    za[1, 8, 1].wait_recv()
    zm[0, 8].wait_recv()
    select(1)
    loads[0].wait()
    loads[1].wait()
    for g in range(2):
        for j in range(1, NX):
            xa[g, j].wait_recv()
        parts(g)
        if g == 0:
            y_step(0, 0)
    for s in range(NY - 1):
        if s:
            y_step(0, s)
        y_step(1, s)
    activate(0)
    activate(1)
    for k in range(1, 5):
        gather_step(0, k)
        gather_step(1, k)
    loads[2].wait()
    down(0)
    down(1)
    combine(1)
    for k in range(8, 4, -1):
        z_sum(k)
    combine(0)
    for k in range(4, 0, -1):
        z_sum(k)
    for sub in range(2):
        total = pt[place(0), sub * half : (sub + 1) * half, :]
        for way in range(2):
            zr[way, 1, sub].wait_recv()
            total = total + rz[way, 0, sub].astype(F32)
        out[sub * half : (sub + 1) * half, :] = total.astype(BF16)

    for copies in (za, zm, xa, rs, ag, xb, zr):
        for copy in copies.values():
            copy.wait_send()
    for g in range(2):
        for s in range(NY):
            pair(g, s).wait_send()
        for index, sigma in enumerate(order[g]):
            hand(g, index, sigma).wait_send()


def shards(tokens, expert_ids, combine_weights, w_gate, w_up, w_down):
    rows, width = tokens.shape
    hidden = w_gate.shape[2]
    vmem = pl.BlockSpec(memory_space=pltpu.VMEM)
    hbm = pl.BlockSpec(memory_space=pl.ANY)
    dma = pltpu.SemaphoreType.DMA
    return pl.pallas_call(
        body,
        out_shape=jax.ShapeDtypeStruct((rows, width), BF16),
        in_specs=[vmem, vmem, vmem, hbm, hbm, hbm],
        out_specs=vmem,
        scratch_shapes=[
            pltpu.VMEM((width, hidden), BF16),
            pltpu.VMEM((width, hidden), BF16),
            pltpu.VMEM((hidden, width), BF16),
            pltpu.VMEM((16, 64, width), BF16),
            pltpu.VMEM((16, 8, 128), F32),
            pltpu.VMEM((2, 3, 80, width), BF16),
            pltpu.VMEM((2, 4, 80, width), BF16),
            pltpu.VMEM((2, 320, 512), BF16),
            pltpu.VMEM((2, 320, 512), BF16),
            pltpu.VMEM((2, 8, 2, 2, 160, 128), F32),
            pltpu.VMEM((2, 8, 2, 160, 128), F32),
            pltpu.VMEM((2, 7, 2, 160, 128), F32),
            pltpu.VMEM((2, 7, 2, 160, 128), F32),
            pltpu.VMEM((2, 2, 160, hidden), BF16),
            pltpu.VMEM((2, 4, 80, width), BF16),
            pltpu.VMEM((2, 4, 80, width), BF16),
            pltpu.VMEM((16, 64, width), F32),
            pltpu.VMEM((2, 8, 2, 32, width), BF16),
            pltpu.VMEM((2, 8, 2, 32, width), BF16),
            dma((3,)),
            dma,
            dma((2, 8, 2)),
            dma((2, 8, 2)),
            dma((2, 8)),
            dma((2, 8)),
            dma((2, 3)),
            dma((2, 3)),
            dma((2, 8)),
            dma((2, 8)),
            dma((2, 7, 2)),
            dma((2, 7, 2)),
            dma((2, 2, 4)),
            dma((2, 2, 4)),
            dma((2, 8)),
            dma((2, 8)),
            dma((2, 3)),
            dma((2, 3)),
            dma((2, 8, 2)),
            dma((2, 8, 2)),
        ],
        compiler_params=pltpu.CompilerParams(
            collective_id=0, has_side_effects=True, vmem_limit_bytes=60 * 1024 * 1024
        ),
    )(tokens, expert_ids.T, combine_weights.T, w_gate, w_up, w_down)


def solution(mesh):
    placed = (
        P("expert", "dp"),
        P("expert", None),
        P("expert", None),
        P("expert", "dp", None),
        P("expert", "dp", None),
        P("expert", None, "dp"),
    )
    return jax.shard_map(
        shards, mesh=mesh, in_specs=placed, out_specs=P("expert", "dp"), check_vma=False
    )
```

```python
import jax
import jax.numpy as jnp
from jax import lax
from jax.experimental import pallas as pl
from jax.experimental.pallas import tpu as pltpu
from jax.sharding import PartitionSpec as P

CAP = 10
NZ, NX, NY, NS = 16, 4, 8, 2
MESH = pl.DeviceIdType.MESH
F32, BF16 = jnp.float32, jnp.bfloat16


def place(sigma):
    return (sigma + 3) % NZ


def body(
    tok, ids, wts, wg_hbm, wu_hbm, wd_hbm, out,
    wg, wu, wd, blk, meta, xs, xr, wt_hi, wt_lo, part, prx, sb, rr, hid, ob, yb, pt, zs, rz,
    w_sem, za_s, za_r, zm_s, zm_r, xa_s, xa_r, pp_s, pp_r, rs_s, rs_r,
    ag_s, ag_r, ph_s, ph_r, xb_s, xb_r, zr_s, zr_r,
):
    width, padded = tok.shape[1], blk.shape[2]
    d, e = lax.axis_index("dp"), lax.axis_index("expert")
    y, c = d // 2, d % 2
    z, x = e // NX, e % NX

    z_dev = ({"expert": ((z + 1) % NZ) * NX + x}, {"expert": ((z + NZ - 1) % NZ) * NX + x})
    z_two = ({"expert": ((z + 2) % NZ) * NX + x}, {"expert": ((z + NZ - 2) % NZ) * NX + x})
    x_fwd = [None] + [{"expert": z * NX + (x + j) % NX} for j in range(1, NX)]
    x_bwd = [None] + [{"expert": z * NX + (x + NX - j) % NX} for j in range(1, NX)]
    y_dev = ({"dp": ((y + 1) % NY) * 2 + c}, {"dp": ((y + NY - 1) % NY) * 2 + c})
    y_two = ({"dp": ((y + 2) % NY) * 2 + c}, {"dp": ((y + NY - 2) % NY) * 2 + c})
    partner = {"dp": y * 2 + (1 - c)}

    def remote(src, dst, ssem, rsem, dev):
        return pltpu.make_async_remote_copy(
            src_ref=src, dst_ref=dst, send_sem=ssem, recv_sem=rsem, device_id=dev, device_id_type=MESH
        )

    loads = [
        pltpu.make_async_copy(wg_hbm.at[0], wg.at[pl.ds(0, width)], w_sem.at[0]),
        pltpu.make_async_copy(wu_hbm.at[0], wu.at[pl.ds(0, width)], w_sem.at[1]),
        pltpu.make_async_copy(wd_hbm.at[0], wd.at[pl.ds(0, width)], w_sem.at[2]),
    ]
    for load in loads:
        load.start()
    barrier = pltpu.get_barrier_semaphore()
    for dev in (*z_dev, *z_two, *x_fwd[1:], *y_dev, *y_two, partner):
        pl.semaphore_signal(barrier, inc=1, device_id=dev, device_id_type=MESH)

    def routing():
        e_iota = lax.broadcasted_iota(jnp.int32, (64, 64), 0)
        t_iota = lax.broadcasted_iota(jnp.int32, (64, 64), 1)
        named = jnp.zeros((64, 64), F32)
        for k in range(8):
            named = named + (e_iota == ids[k : k + 1, :]).astype(F32)
        before = jnp.dot(
            named.astype(BF16), (e_iota < t_iota).astype(F32).astype(BF16), preferred_element_type=F32
        )
        for k in range(8):
            row = ids[k : k + 1, :]
            position = jnp.sum(jnp.where(e_iota == row, before, 0.0), axis=0, keepdims=True)
            meta[place(0), k : k + 1, 0:64] = row.astype(F32) * 16.0 + position
        meta[place(0), :, 64:128] = wts[...]

    blk[place(0)] = jnp.zeros((64, padded), BF16)
    blk[place(0), :, 0:width] = tok[...]
    for weight in (wg, wu, wd):
        weight[width:padded, :] = jnp.zeros((padded - width, weight.shape[1]), BF16)
    pl.semaphore_wait(barrier, 12)

    def ring_place(way, k):
        return place(k if way == 0 else (NZ - k) % NZ)

    half = 64 // NS
    za, zm = {}, {}
    for way in range(2):
        for k in range(1, 9):
            for sub in range(NS):
                if k == 8 and sub * 2 // NS != way:
                    continue
                rows = pl.ds(sub * half, half)
                src = blk.at[ring_place(way, (k - 1) // 2 * 2), rows]
                za[way, k, sub] = remote(
                    src, blk.at[ring_place(way, k), rows], za_s.at[way, k - 1, sub], za_r.at[way, k - 1, sub],
                    (z_dev if k % 2 else z_two)[way],
                )
            if k < 8 or way == 0:
                zm[way, k] = remote(
                    meta.at[ring_place(way, (k - 1) // 2 * 2)], meta.at[ring_place(way, k)],
                    zm_s.at[way, k - 1], zm_r.at[way, k - 1], (z_dev if k % 2 else z_two)[way],
                )

    def z_go(k):
        for sub in range(NS):
            for way in range(2):
                if k:
                    za[way, k, sub].wait_recv()
                for onward in (k + 2, k + 1):
                    if (way, onward, sub) in za:
                        za[way, onward, sub].start()
        if k == 0:
            routing()
        for way in range(2):
            if k:
                zm[way, k].wait_recv()
            for onward in (k + 2, k + 1):
                if (way, onward) in zm:
                    zm[way, onward].start()

    def z_take(*ks):
        for k in ks:
            for way in range(2):
                for sub in range(NS):
                    if (way, k, sub) in za:
                        za[way, k, sub].wait_recv()
                if (way, k) in zm:
                    zm[way, k].wait_recv()

    lane = lax.broadcasted_iota(jnp.int32, (8, 128), 1)
    row_iota = lax.broadcasted_iota(jnp.int32, (80, 512), 0).astype(F32)
    src_row = (lax.broadcasted_iota(jnp.int32, (1, 512), 1) // 64 * CAP).astype(F32)
    xa = {}
    for g in range(2):
        for j in range(1, NX):
            xa[g, j] = remote(xs.at[g, j - 1], xr.at[g, j], xa_s.at[g, j - 1], xa_r.at[g, j - 1], x_fwd[j])

    def select(g):
        codes, weights = [], []
        for s in range(0, 8, 2):
            a, b = meta[8 * g + s], meta[8 * g + s + 1]
            codes.append(jnp.where(lane < 64, a, pltpu.roll(b, 64, 1)))
            weights.append(jnp.where(lane < 64, pltpu.roll(a, 64, 1), b))
        code = jnp.concatenate(codes, axis=1)
        weight = jnp.concatenate(weights, axis=1)
        rows = blk[8 * g : 8 * g + 8].reshape(512, padded)
        for j in (2, 1, 3, 0):
            base = ((z * NX + (x + j) % NX) * 16).astype(F32)
            own = code - base
            hit = jnp.logical_and(own >= 0.0, own < 16.0)
            slot = jnp.max(jnp.where(hit, own, -1.0), axis=0, keepdims=True)
            share = jnp.sum(jnp.where(hit, weight, 0.0), axis=0, keepdims=True)
            target = jnp.where(slot >= 0.0, slot + src_row, -1.0)
            chosen = row_iota == target
            pick = jnp.dot(chosen.astype(F32).astype(BF16), rows, preferred_element_type=F32).astype(BF16)
            if j:
                xs[g, j - 1] = pick
                xa[g, j].start()
            else:
                xr[g, 0] = pick
            scaled = jnp.where(chosen, share, 0.0)
            high = scaled.astype(BF16)
            wt_hi[g, 80 * j : 80 * j + 80, :] = high
            wt_lo[g, 80 * j : 80 * j + 80, :] = (scaled - high.astype(F32)).astype(BF16)

    def pair(g, s):
        return remote(part.at[g, s, 1 - c], prx.at[g, s], pp_s.at[g, s], pp_r.at[g, s], partner)

    def parts(g, low, high):
        rows = xr[g].reshape(320, padded)

        def piece(s, carry):
            offset = (4 - (s + 1) // 2) * (2 * (s % 2) - 1)
            at = pl.multiple_of((y + NY + offset) % NY * 128, 128)
            gate = jnp.dot(rows, wg[:, pl.ds(at, 128)], preferred_element_type=F32)
            up = jnp.dot(rows, wu[:, pl.ds(at, 128)], preferred_element_type=F32)
            part[g, s, :, 0] = gate.reshape(2, 160, 128)
            part[g, s, :, 1] = up.reshape(2, 160, 128)
            pair(g, s).start()
            return carry

        lax.fori_loop(low, high, piece, 0)

    rs = {}
    for g in range(2):
        for way in range(2):
            for k in range(1, 5):
                for m in range(2):
                    if k == 4 and m != way:
                        continue
                    rs[g, way, k, m] = remote(
                        sb.at[g, way, k - 1, m], rr.at[g, way, k - 1, m],
                        rs_s.at[g, way, k - 1, m], rs_r.at[g, way, k - 1, m], y_dev[way],
                    )

    def y_step(g, k):
        for s in (0,) if k == 4 else (7 - 2 * k, 8 - 2 * k):
            pair(g, s).wait_recv()
        for m in range(2):
            for way in range(2):
                if (g, way, k, m) not in rs:
                    continue
                s = 0 if k == 4 else 7 - 2 * k + way
                value = part[g, s, c, m] + prx[g, s, m]
                if (g, way, k + 1, m) in rs:
                    rs[g, way, k + 1, m].wait_recv()
                    value = value + rr[g, way, k, m]
                sb[g, way, k - 1, m] = value
                rs[g, way, k, m].start()

    def unit(k):
        return (y + 2 * NY - k) % NY

    ag, order = {}, {}
    for g in range(2):
        for way in range(2):
            sign = 1 if way == 0 else -1
            for near in range(1, 5):
                if near == 4 and way != g:
                    continue
                held = hid.at[g, c, unit(0 if near < 3 else 2 * sign)]
                ag[g, sign * near] = remote(
                    held, held, ag_s.at[g, sign * near + 4], ag_r.at[g, sign * near + 4],
                    (y_dev if near % 2 else y_two)[way],
                )
        order[g] = [0, 1, -1, 2, -2, 3, -3, 4 if g == 0 else -4]

    def arrived(g, sigma):
        there = hid.at[g, c, unit(sigma)]
        dev = y_dev[0 if sigma > 0 else 1]
        return remote(there, there, ag_s.at[g, sigma + 4], ag_r.at[g, sigma + 4], dev)

    def hand(g, index, sigma):
        there = hid.at[g, c, unit(sigma)]
        return remote(there, there, ph_s.at[g, index], ph_r.at[g, index], partner)

    def received(g, index, sigma):
        there = hid.at[g, 1 - c, unit(sigma)]
        return remote(there, there, ph_s.at[g, index], ph_r.at[g, index], partner)

    def activate(g):
        pair(g, NY - 1).wait_recv()
        sums = []
        for m in range(2):
            value = part[g, NY - 1, c, m] + prx[g, NY - 1, m]
            for way in range(2):
                rs[g, way, 1, m].wait_recv()
                value = value + rr[g, way, 0, m]
            sums.append(value)
        gate, up = sums
        hid[g, c, unit(0)] = (gate / (1.0 + jnp.exp(-gate)) * up).astype(BF16)
        for sigma in (2, -2, 1, -1):
            ag[g, sigma].start()
        hand(g, 0, 0).start()

    def gather(g, low, high):
        for index in range(low, high):
            sigma = order[g][index]
            arrived(g, sigma).wait_recv()
            if abs(sigma) == 2:
                for onward in (sigma * 2, sigma * 3 // 2):
                    if (g, onward) in ag:
                        ag[g, onward].start()
            hand(g, index, sigma).start()

    xb = {}
    for g in range(2):
        for j in range(1, NX):
            xb[g, j] = remote(ob.at[g, j], yb.at[g, j], xb_s.at[g, j - 1], xb_r.at[g, j - 1], x_bwd[j])

    def down(g):
        for index, sigma in enumerate(order[g]):
            received(g, index, sigma).wait_recv()
        for h in (1, 0):
            rows = jnp.concatenate([hid[g, h, u] for u in range(NY)], axis=1)
            res = lax.dot_general(rows, wd[...], (((1,), (1,)), ((), ())), preferred_element_type=F32)
            res = res.astype(BF16).reshape(2, 80, padded)
            if h:
                ob[g, 2] = res[0]
                xb[g, 2].start()
                ob[g, 3] = res[1]
                xb[g, 3].start()
            else:
                ob[g, 1] = res[1]
                xb[g, 1].start()
                yb[g, 0] = res[0]

    def combine(g):
        for j in range(1, NX):
            xb[g, j].wait_recv()
        rows = yb[g].reshape(320, padded)
        dims = (((0,), (0,)), ((), ()))
        res = lax.dot_general(wt_hi[g], rows, dims, preferred_element_type=F32)
        res = res + lax.dot_general(wt_lo[g], rows, dims, preferred_element_type=F32)
        pt[8 * g : 8 * g + 8] = res.reshape(8, 64, padded)

    zr = {}
    for way in range(2):
        for k in range(1, 9):
            for sub in range(NS):
                if k == 8 and sub * 2 // NS != way:
                    continue
                zr[way, k, sub] = remote(
                    zs.at[way, k - 1, sub], rz.at[way, k - 1, sub], zr_s.at[way, k - 1, sub], zr_r.at[way, k - 1, sub],
                    (z_dev if k % 2 else z_two)[way],
                )

    def z_sum(k):
        for sub in range(NS):
            for way in range(2):
                if (way, k, sub) not in zr:
                    continue
                at = ring_place(1 - way, k)
                value = pt[at, sub * half : (sub + 1) * half, :]
                for before in (k + 1, k + 2):
                    if k % 2 == 0 and (way, before, sub) in zr:
                        zr[way, before, sub].wait_recv()
                        value = value + rz[way, before - 1, sub].astype(F32)
                zs[way, k - 1, sub] = value.astype(BF16)
                zr[way, k, sub].start()

    def sent(*groups):
        for copies in groups:
            for copy in copies:
                copy.wait_send()

    z_go(0)
    z_go(2)
    z_go(4)
    z_take(1, 3)
    select(0)
    loads[0].wait()
    loads[1].wait()
    for j in range(1, NX):
        xa[0, j].wait_recv()
    parts(0, 0, 3)
    z_go(6)
    y_step(0, 4)
    parts(0, 3, 5)
    y_step(0, 3)
    parts(0, 5, 8)
    z_take(5, 7, 8)
    select(1)
    y_step(0, 2)
    for j in range(1, NX):
        xa[1, j].wait_recv()
    parts(1, 0, 3)
    y_step(1, 4)
    y_step(0, 1)
    parts(1, 3, 5)
    y_step(1, 3)
    activate(0)
    parts(1, 5, 8)
    y_step(1, 2)
    gather(0, 1, 5)
    y_step(1, 1)
    gather(0, 5, 8)
    activate(1)
    loads[2].wait()
    down(0)
    sent(za.values(), zm.values(), xa.values())
    gather(1, 1, 5)
    sent(pair(g, s) for g in range(2) for s in range(NY))
    gather(1, 5, 8)
    down(1)
    combine(0)
    z_sum(3)
    z_sum(1)
    sent(rs.values(), ag.values())
    sent(hand(g, index, sigma) for g in range(2) for index, sigma in enumerate(order[g]))
    combine(1)
    for k in (8, 7, 5, 6, 4, 2):
        z_sum(k)
    sent(xb.values())
    for sub in range(NS):
        total = pt[place(0), sub * half : (sub + 1) * half, :]
        for way in range(2):
            for k in (1, 2):
                zr[way, k, sub].wait_recv()
                total = total + rz[way, k - 1, sub].astype(F32)
        out[sub * half : (sub + 1) * half, :] = total[:, 0:width].astype(BF16)
    sent(zr.values())


def shards(tokens, expert_ids, combine_weights, w_gate, w_up, w_down):
    rows, width = tokens.shape
    padded = pl.cdiv(width, 128) * 128
    hidden = w_gate.shape[2]
    vmem = pl.BlockSpec(memory_space=pltpu.VMEM)
    hbm = pl.BlockSpec(memory_space=pl.ANY)
    dma = pltpu.SemaphoreType.DMA
    return pl.pallas_call(
        body,
        out_shape=jax.ShapeDtypeStruct((rows, width), BF16),
        in_specs=[vmem, vmem, vmem, hbm, hbm, hbm],
        out_specs=vmem,
        scratch_shapes=[
            pltpu.VMEM((padded, hidden), BF16),
            pltpu.VMEM((padded, hidden), BF16),
            pltpu.VMEM((padded, hidden), BF16),
            pltpu.VMEM((16, 64, padded), BF16),
            pltpu.VMEM((16, 8, 128), F32),
            pltpu.VMEM((2, 3, 80, padded), BF16),
            pltpu.VMEM((2, 4, 80, padded), BF16),
            pltpu.VMEM((2, 320, 512), BF16),
            pltpu.VMEM((2, 320, 512), BF16),
            pltpu.VMEM((2, 8, 2, 2, 160, 128), F32),
            pltpu.VMEM((2, 8, 2, 160, 128), F32),
            pltpu.VMEM((2, 2, 4, 2, 160, 128), F32),
            pltpu.VMEM((2, 2, 4, 2, 160, 128), F32),
            pltpu.VMEM((2, 2, 8, 160, 128), BF16),
            pltpu.VMEM((2, 4, 80, padded), BF16),
            pltpu.VMEM((2, 4, 80, padded), BF16),
            pltpu.VMEM((16, 64, padded), F32),
            pltpu.VMEM((2, 8, NS, 64 // NS, padded), BF16),
            pltpu.VMEM((2, 8, NS, 64 // NS, padded), BF16),
            dma((3,)),
            dma((2, 8, NS)),
            dma((2, 8, NS)),
            dma((2, 8)),
            dma((2, 8)),
            dma((2, 3)),
            dma((2, 3)),
            dma((2, 8)),
            dma((2, 8)),
            dma((2, 2, 4, 2)),
            dma((2, 2, 4, 2)),
            dma((2, 9)),
            dma((2, 9)),
            dma((2, 8)),
            dma((2, 8)),
            dma((2, 3)),
            dma((2, 3)),
            dma((2, 8, NS)),
            dma((2, 8, NS)),
        ],
        compiler_params=pltpu.CompilerParams(
            collective_id=0, has_side_effects=True, vmem_limit_bytes=60 * 1024 * 1024
        ),
    )(tokens, expert_ids.T, combine_weights.T, w_gate, w_up, w_down.transpose(0, 2, 1))


def solution(mesh):
    placed = (
        P("expert", "dp"),
        P("expert", None),
        P("expert", None),
        P("expert", "dp", None),
        P("expert", "dp", None),
        P("expert", None, "dp"),
    )
    return jax.shard_map(
        shards, mesh=mesh, in_specs=placed, out_specs=P("expert", "dp"), check_vma=False
    )
```

```python
import jax
import jax.numpy as jnp
from jax import lax
from jax.experimental import pallas as pl
from jax.experimental.pallas import tpu as pltpu
from jax.sharding import PartitionSpec as P

CAP = 10
NZ, NX, NY, NS = 16, 4, 8, 2
MESH = pl.DeviceIdType.MESH
F32, BF16 = jnp.float32, jnp.bfloat16


def place(sigma):
    return (sigma + 3) % NZ


def body(
    tok, ids, wts, wg_hbm, wu_hbm, wd_hbm, out,
    wg, wu, wd, blk, meta, xs, xr, wt_hi, wt_lo, part, prx, sb, rr, hid, ob, yb, pt, zs, rz,
    w_sem, za_s, za_r, zm_s, zm_r, xa_s, xa_r, pp_s, pp_r, rs_s, rs_r,
    ag_s, ag_r, ph_s, ph_r, xb_s, xb_r, zr_s, zr_r,
):
    width, padded = tok.shape[1], blk.shape[2]
    d, e = lax.axis_index("dp"), lax.axis_index("expert")
    y, c = d // 2, d % 2
    z, x = e // NX, e % NX

    z_dev = ({"expert": ((z + 1) % NZ) * NX + x}, {"expert": ((z + NZ - 1) % NZ) * NX + x})
    z_two = ({"expert": ((z + 2) % NZ) * NX + x}, {"expert": ((z + NZ - 2) % NZ) * NX + x})
    x_fwd = [None] + [{"expert": z * NX + (x + j) % NX} for j in range(1, NX)]
    x_bwd = [None] + [{"expert": z * NX + (x + NX - j) % NX} for j in range(1, NX)]
    y_dev = ({"dp": ((y + 1) % NY) * 2 + c}, {"dp": ((y + NY - 1) % NY) * 2 + c})
    y_two = ({"dp": ((y + 2) % NY) * 2 + c}, {"dp": ((y + NY - 2) % NY) * 2 + c})
    partner = {"dp": y * 2 + (1 - c)}

    def remote(src, dst, ssem, rsem, dev):
        return pltpu.make_async_remote_copy(
            src_ref=src, dst_ref=dst, send_sem=ssem, recv_sem=rsem, device_id=dev, device_id_type=MESH
        )

    loads = [
        pltpu.make_async_copy(wg_hbm.at[0], wg.at[pl.ds(0, width)], w_sem.at[0]),
        pltpu.make_async_copy(wu_hbm.at[0], wu.at[pl.ds(0, width)], w_sem.at[1]),
        pltpu.make_async_copy(wd_hbm.at[0], wd.at[pl.ds(0, width)], w_sem.at[2]),
    ]
    for load in loads:
        load.start()
    barrier = pltpu.get_barrier_semaphore()
    for dev in (*z_dev, *z_two, *x_fwd[1:], *y_dev, *y_two, partner):
        pl.semaphore_signal(barrier, inc=1, device_id=dev, device_id_type=MESH)

    def routing():
        e_iota = lax.broadcasted_iota(jnp.int32, (64, 64), 0)
        t_iota = lax.broadcasted_iota(jnp.int32, (64, 64), 1)
        named = jnp.zeros((64, 64), F32)
        for k in range(8):
            named = named + (e_iota == ids[k : k + 1, :]).astype(F32)
        before = jnp.dot(
            named.astype(BF16), (e_iota < t_iota).astype(F32).astype(BF16), preferred_element_type=F32
        )
        for k in range(8):
            row = ids[k : k + 1, :]
            position = jnp.sum(jnp.where(e_iota == row, before, 0.0), axis=0, keepdims=True)
            meta[place(0), k : k + 1, 0:64] = row.astype(F32) * 16.0 + position
        meta[place(0), :, 64:128] = wts[...]

    blk[place(0)] = jnp.zeros((64, padded), BF16)
    blk[place(0), :, 0:width] = tok[...]
    for weight in (wg, wu, wd):
        weight[width:padded, :] = jnp.zeros((padded - width, weight.shape[1]), BF16)
    pl.semaphore_wait(barrier, 12)

    def ring_place(way, k):
        return place(k if way == 0 else (NZ - k) % NZ)

    half = 64 // NS
    za, zm = {}, {}
    for way in range(2):
        for k in range(1, 9):
            for sub in range(NS):
                if k == 8 and sub * 2 // NS != way:
                    continue
                rows = pl.ds(sub * half, half)
                src = blk.at[ring_place(way, (k - 1) // 2 * 2), rows]
                za[way, k, sub] = remote(
                    src, blk.at[ring_place(way, k), rows], za_s.at[way, k - 1, sub], za_r.at[way, k - 1, sub],
                    (z_dev if k % 2 else z_two)[way],
                )
            if k < 8 or way == 0:
                zm[way, k] = remote(
                    meta.at[ring_place(way, (k - 1) // 2 * 2)], meta.at[ring_place(way, k)],
                    zm_s.at[way, k - 1], zm_r.at[way, k - 1], (z_dev if k % 2 else z_two)[way],
                )

    def z_go(k):
        for sub in range(NS):
            for way in range(2):
                if k:
                    za[way, k, sub].wait_recv()
                for onward in (k + 2, k + 1):
                    if (way, onward, sub) in za:
                        za[way, onward, sub].start()
        if k == 0:
            routing()
        for way in range(2):
            if k:
                zm[way, k].wait_recv()
            for onward in (k + 2, k + 1):
                if (way, onward) in zm:
                    zm[way, onward].start()

    def z_take(*ks):
        for k in ks:
            for way in range(2):
                for sub in range(NS):
                    if (way, k, sub) in za:
                        za[way, k, sub].wait_recv()
                if (way, k) in zm:
                    zm[way, k].wait_recv()

    lane = lax.broadcasted_iota(jnp.int32, (8, 128), 1)
    row_iota = lax.broadcasted_iota(jnp.int32, (80, 512), 0).astype(F32)
    src_row = (lax.broadcasted_iota(jnp.int32, (1, 512), 1) // 64 * CAP).astype(F32)
    xa = {}
    for g in range(2):
        for j in range(1, NX):
            xa[g, j] = remote(xs.at[g, j - 1], xr.at[g, j], xa_s.at[g, j - 1], xa_r.at[g, j - 1], x_fwd[j])

    def select(g):
        codes, weights = [], []
        for s in range(0, 8, 2):
            a, b = meta[8 * g + s], meta[8 * g + s + 1]
            codes.append(jnp.where(lane < 64, a, pltpu.roll(b, 64, 1)))
            weights.append(jnp.where(lane < 64, pltpu.roll(a, 64, 1), b))
        code = jnp.concatenate(codes, axis=1)
        weight = jnp.concatenate(weights, axis=1)
        rows = blk[8 * g : 8 * g + 8].reshape(512, padded)
        for j in (2, 1, 3, 0):
            base = ((z * NX + (x + j) % NX) * 16).astype(F32)
            own = code - base
            hit = jnp.logical_and(own >= 0.0, own < 16.0)
            slot = jnp.max(jnp.where(hit, own, -1.0), axis=0, keepdims=True)
            share = jnp.sum(jnp.where(hit, weight, 0.0), axis=0, keepdims=True)
            target = jnp.where(slot >= 0.0, slot + src_row, -1.0)
            chosen = row_iota == target
            pick = jnp.dot(chosen.astype(F32).astype(BF16), rows, preferred_element_type=F32).astype(BF16)
            if j:
                xs[g, j - 1] = pick
                xa[g, j].start()
            else:
                xr[g, 0] = pick
            scaled = jnp.where(chosen, share, 0.0)
            high = scaled.astype(BF16)
            wt_hi[g, 80 * j : 80 * j + 80, :] = high
            wt_lo[g, 80 * j : 80 * j + 80, :] = (scaled - high.astype(F32)).astype(BF16)

    def pair(g, s):
        return remote(part.at[g, s, 1 - c], prx.at[g, s], pp_s.at[g, s], pp_r.at[g, s], partner)

    def parts(g, low, high):
        rows = xr[g].reshape(320, padded)

        def piece(s, carry):
            offset = (4 - (s + 1) // 2) * (2 * (s % 2) - 1)
            at = pl.multiple_of((y + NY + offset) % NY * 128, 128)
            gate = jnp.dot(rows, wg[:, pl.ds(at, 128)], preferred_element_type=F32)
            up = jnp.dot(rows, wu[:, pl.ds(at, 128)], preferred_element_type=F32)
            part[g, s, :, 0] = gate.reshape(2, 160, 128)
            part[g, s, :, 1] = up.reshape(2, 160, 128)
            pair(g, s).start()
            return carry

        lax.fori_loop(low, high, piece, 0)

    rs = {}
    for g in range(2):
        for way in range(2):
            for k in range(1, 5):
                for m in range(2):
                    if k == 4 and m != way:
                        continue
                    rs[g, way, k, m] = remote(
                        sb.at[g, way, k - 1, m], rr.at[g, way, k - 1, m],
                        rs_s.at[g, way, k - 1, m], rs_r.at[g, way, k - 1, m], y_dev[way],
                    )

    def y_step(g, k):
        for s in (0,) if k == 4 else (7 - 2 * k, 8 - 2 * k):
            pair(g, s).wait_recv()
        for m in range(2):
            for way in range(2):
                if (g, way, k, m) not in rs:
                    continue
                s = 0 if k == 4 else 7 - 2 * k + way
                value = part[g, s, c, m] + prx[g, s, m]
                if (g, way, k + 1, m) in rs:
                    rs[g, way, k + 1, m].wait_recv()
                    value = value + rr[g, way, k, m]
                sb[g, way, k - 1, m] = value
                rs[g, way, k, m].start()

    def unit(k):
        return (y + 2 * NY - k) % NY

    ag, order = {}, {}
    for g in range(2):
        for way in range(2):
            sign = 1 if way == 0 else -1
            for near in range(1, 5):
                if near == 4 and way != g:
                    continue
                held = hid.at[g, c, unit(0 if near < 3 else 2 * sign)]
                ag[g, sign * near] = remote(
                    held, held, ag_s.at[g, sign * near + 4], ag_r.at[g, sign * near + 4],
                    (y_dev if near % 2 else y_two)[way],
                )
        order[g] = [0, 1, -1, 2, -2, 3, -3, 4 if g == 0 else -4]

    def arrived(g, sigma):
        there = hid.at[g, c, unit(sigma)]
        dev = y_dev[0 if sigma > 0 else 1]
        return remote(there, there, ag_s.at[g, sigma + 4], ag_r.at[g, sigma + 4], dev)

    def hand(g, index, sigma):
        there = hid.at[g, c, unit(sigma)]
        return remote(there, there, ph_s.at[g, index], ph_r.at[g, index], partner)

    def received(g, index, sigma):
        there = hid.at[g, 1 - c, unit(sigma)]
        return remote(there, there, ph_s.at[g, index], ph_r.at[g, index], partner)

    def activate(g):
        pair(g, NY - 1).wait_recv()
        sums = []
        for m in range(2):
            value = part[g, NY - 1, c, m] + prx[g, NY - 1, m]
            for way in range(2):
                rs[g, way, 1, m].wait_recv()
                value = value + rr[g, way, 0, m]
            sums.append(value)
        gate, up = sums
        hid[g, c, unit(0)] = (gate / (1.0 + jnp.exp(-gate)) * up).astype(BF16)
        for sigma in (2, -2, 1, -1):
            ag[g, sigma].start()
        hand(g, 0, 0).start()

    def gather(g, low, high):
        for index in range(low, high):
            sigma = order[g][index]
            arrived(g, sigma).wait_recv()
            if abs(sigma) == 2:
                for onward in (sigma * 2, sigma * 3 // 2):
                    if (g, onward) in ag:
                        ag[g, onward].start()
            hand(g, index, sigma).start()

    xb = {}
    for g in range(2):
        for j in range(1, NX):
            xb[g, j] = remote(ob.at[g, j], yb.at[g, j], xb_s.at[g, j - 1], xb_r.at[g, j - 1], x_bwd[j])

    def down(g):
        for index, sigma in enumerate(order[g]):
            received(g, index, sigma).wait_recv()
        for h in (1, 0):
            rows = jnp.concatenate([hid[g, h, u] for u in range(NY)], axis=1)
            res = lax.dot_general(rows, wd[...], (((1,), (1,)), ((), ())), preferred_element_type=F32)
            res = res.astype(BF16).reshape(2, 80, padded)
            if h:
                ob[g, 2] = res[0]
                xb[g, 2].start()
                ob[g, 3] = res[1]
                xb[g, 3].start()
            else:
                ob[g, 1] = res[1]
                xb[g, 1].start()
                yb[g, 0] = res[0]

    def combine(g):
        for j in range(1, NX):
            xb[g, j].wait_recv()
        rows = yb[g].reshape(320, padded)
        dims = (((0,), (0,)), ((), ()))
        res = lax.dot_general(wt_hi[g], rows, dims, preferred_element_type=F32)
        res = res + lax.dot_general(wt_lo[g], rows, dims, preferred_element_type=F32)
        pt[8 * g : 8 * g + 8] = res.reshape(8, 64, padded)

    low = lax.broadcasted_iota(jnp.int32, (half // 2, 128), 1) < 64

    def pack(to, value):
        for tile in range(3):
            to[tile * half : (tile + 1) * half, :] = value[:, 128 * tile : 128 * tile + 128].astype(BF16)
        rest = value[:, 384:512]
        both = jnp.where(low, rest[: half // 2], pltpu.roll(rest[half // 2 :], 64, 1))
        to[3 * half :, :] = both.astype(BF16)

    def unpack(value):
        value = value.astype(F32)
        both = value[3 * half :]
        rest = jnp.concatenate(
            [jnp.where(low, both, 0.0), jnp.where(low, pltpu.roll(both, 64, 1), 0.0)], axis=0
        )
        return jnp.concatenate([value[tile * half : (tile + 1) * half] for tile in range(3)] + [rest], axis=1)

    zr = {}
    for way in range(2):
        for k in range(1, 9):
            for sub in range(NS):
                if k == 8 and sub * 2 // NS != way:
                    continue
                zr[way, k, sub] = remote(
                    zs.at[way, k - 1, sub], rz.at[way, k - 1, sub], zr_s.at[way, k - 1, sub], zr_r.at[way, k - 1, sub],
                    (z_dev if k % 2 else z_two)[way],
                )

    def z_sum(k):
        for sub in range(NS):
            for way in range(2):
                if (way, k, sub) not in zr:
                    continue
                at = ring_place(1 - way, k)
                value = pt[at, sub * half : (sub + 1) * half, :]
                for before in (k + 1, k + 2):
                    if k % 2 == 0 and (way, before, sub) in zr:
                        zr[way, before, sub].wait_recv()
                        value = value + unpack(rz[way, before - 1, sub])
                pack(zs.at[way, k - 1, sub], value)
                zr[way, k, sub].start()

    def sent(*groups):
        for copies in groups:
            for copy in copies:
                copy.wait_send()

    z_go(0)
    z_go(2)
    z_go(4)
    z_take(1, 3)
    select(0)
    loads[0].wait()
    loads[1].wait()
    for j in range(1, NX):
        xa[0, j].wait_recv()
    parts(0, 0, 1)
    z_go(6)
    y_step(0, 4)
    parts(0, 1, 5)
    z_take(5, 7, 8)
    select(1)
    y_step(0, 3)
    parts(0, 5, 8)
    for j in range(1, NX):
        xa[1, j].wait_recv()
    parts(1, 0, 1)
    y_step(0, 2)
    y_step(1, 4)
    parts(1, 1, 5)
    y_step(0, 1)
    y_step(1, 3)
    parts(1, 5, 8)
    activate(0)
    y_step(1, 2)
    gather(0, 1, 5)
    y_step(1, 1)
    gather(0, 5, 8)
    activate(1)
    loads[2].wait()
    down(0)
    sent(za.values(), zm.values(), xa.values())
    gather(1, 1, 5)
    sent(pair(g, s) for g in range(2) for s in range(NY))
    gather(1, 5, 8)
    down(1)
    combine(0)
    z_sum(3)
    z_sum(1)
    sent(rs.values(), ag.values())
    sent(hand(g, index, sigma) for g in range(2) for index, sigma in enumerate(order[g]))
    combine(1)
    for k in (8, 7, 5, 6, 4, 2):
        z_sum(k)
    sent(xb.values())
    for sub in range(NS):
        total = pt[place(0), sub * half : (sub + 1) * half, :]
        for way in range(2):
            for k in (1, 2):
                zr[way, k, sub].wait_recv()
                total = total + unpack(rz[way, k - 1, sub])
        out[sub * half : (sub + 1) * half, :] = total[:, 0:width].astype(BF16)
    sent(zr.values())


def shards(tokens, expert_ids, combine_weights, w_gate, w_up, w_down):
    rows, width = tokens.shape
    padded = pl.cdiv(width, 128) * 128
    hidden = w_gate.shape[2]
    vmem = pl.BlockSpec(memory_space=pltpu.VMEM)
    hbm = pl.BlockSpec(memory_space=pl.ANY)
    dma = pltpu.SemaphoreType.DMA
    return pl.pallas_call(
        body,
        out_shape=jax.ShapeDtypeStruct((rows, width), BF16),
        in_specs=[vmem, vmem, vmem, hbm, hbm, hbm],
        out_specs=vmem,
        scratch_shapes=[
            pltpu.VMEM((padded, hidden), BF16),
            pltpu.VMEM((padded, hidden), BF16),
            pltpu.VMEM((padded, hidden), BF16),
            pltpu.VMEM((16, 64, padded), BF16),
            pltpu.VMEM((16, 8, 128), F32),
            pltpu.VMEM((2, 3, 80, padded), BF16),
            pltpu.VMEM((2, 4, 80, padded), BF16),
            pltpu.VMEM((2, 320, 512), BF16),
            pltpu.VMEM((2, 320, 512), BF16),
            pltpu.VMEM((2, 8, 2, 2, 160, 128), F32),
            pltpu.VMEM((2, 8, 2, 160, 128), F32),
            pltpu.VMEM((2, 2, 4, 2, 160, 128), F32),
            pltpu.VMEM((2, 2, 4, 2, 160, 128), F32),
            pltpu.VMEM((2, 2, 8, 160, 128), BF16),
            pltpu.VMEM((2, 4, 80, padded), BF16),
            pltpu.VMEM((2, 4, 80, padded), BF16),
            pltpu.VMEM((16, 64, padded), F32),
            pltpu.VMEM((2, 8, NS, 64 // NS * 7 // 2, 128), BF16),
            pltpu.VMEM((2, 8, NS, 64 // NS * 7 // 2, 128), BF16),
            dma((3,)),
            dma((2, 8, NS)),
            dma((2, 8, NS)),
            dma((2, 8)),
            dma((2, 8)),
            dma((2, 3)),
            dma((2, 3)),
            dma((2, 8)),
            dma((2, 8)),
            dma((2, 2, 4, 2)),
            dma((2, 2, 4, 2)),
            dma((2, 9)),
            dma((2, 9)),
            dma((2, 8)),
            dma((2, 8)),
            dma((2, 3)),
            dma((2, 3)),
            dma((2, 8, NS)),
            dma((2, 8, NS)),
        ],
        compiler_params=pltpu.CompilerParams(
            collective_id=0, has_side_effects=True, vmem_limit_bytes=60 * 1024 * 1024
        ),
    )(tokens, expert_ids.T, combine_weights.T, w_gate, w_up, w_down.transpose(0, 2, 1))


def solution(mesh):
    placed = (
        P("expert", "dp"),
        P("expert", None),
        P("expert", None),
        P("expert", "dp", None),
        P("expert", "dp", None),
        P("expert", None, "dp"),
    )
    return jax.shard_map(
        shards, mesh=mesh, in_specs=placed, out_specs=P("expert", "dp"), check_vma=False
    )
```

```python
import jax
import jax.numpy as jnp
from jax import lax
from jax.experimental import pallas as pl
from jax.experimental.pallas import tpu as pltpu
from jax.sharding import PartitionSpec as P

CAP = 10
NZ, NX, NY, NS = 16, 4, 8, 2
MESH = pl.DeviceIdType.MESH
F32, BF16 = jnp.float32, jnp.bfloat16


def place(sigma):
    return (sigma + 3) % NZ


def body(
    tok, ids, wts, wg_hbm, wu_hbm, wd_hbm, out,
    wg, wu, wd, blk, meta, xs, xr, wt_hi, wt_lo, part, prx, sb, rr, sb16, rr16, hid, ob, yb, pt, zs, rz,
    w_sem, za_s, za_r, zm_s, zm_r, xa_s, xa_r, pp_s, pp_r, rs_s, rs_r,
    ag_s, ag_r, ph_s, ph_r, xb_s, xb_r, zr_s, zr_r,
):
    width, padded = tok.shape[1], blk.shape[2]
    d, e = lax.axis_index("dp"), lax.axis_index("expert")
    y, c = d // 2, d % 2
    z, x = e // NX, e % NX

    z_dev = ({"expert": ((z + 1) % NZ) * NX + x}, {"expert": ((z + NZ - 1) % NZ) * NX + x})
    z_two = ({"expert": ((z + 2) % NZ) * NX + x}, {"expert": ((z + NZ - 2) % NZ) * NX + x})
    x_fwd = [None] + [{"expert": z * NX + (x + j) % NX} for j in range(1, NX)]
    x_bwd = [None] + [{"expert": z * NX + (x + NX - j) % NX} for j in range(1, NX)]
    y_dev = ({"dp": ((y + 1) % NY) * 2 + c}, {"dp": ((y + NY - 1) % NY) * 2 + c})
    y_two = ({"dp": ((y + 2) % NY) * 2 + c}, {"dp": ((y + NY - 2) % NY) * 2 + c})
    partner = {"dp": y * 2 + (1 - c)}

    def remote(src, dst, ssem, rsem, dev):
        return pltpu.make_async_remote_copy(
            src_ref=src, dst_ref=dst, send_sem=ssem, recv_sem=rsem, device_id=dev, device_id_type=MESH
        )

    loads = [
        pltpu.make_async_copy(wg_hbm.at[0], wg.at[pl.ds(0, width)], w_sem.at[0]),
        pltpu.make_async_copy(wu_hbm.at[0], wu.at[pl.ds(0, width)], w_sem.at[1]),
        pltpu.make_async_copy(wd_hbm.at[0], wd.at[pl.ds(0, width)], w_sem.at[2]),
    ]
    for load in loads:
        load.start()
    barrier = pltpu.get_barrier_semaphore()
    for dev in (*z_dev, *z_two, *x_fwd[1:], *y_dev, *y_two, partner):
        pl.semaphore_signal(barrier, inc=1, device_id=dev, device_id_type=MESH)

    def routing():
        e_iota = lax.broadcasted_iota(jnp.int32, (64, 64), 0)
        t_iota = lax.broadcasted_iota(jnp.int32, (64, 64), 1)
        named = jnp.zeros((64, 64), F32)
        for k in range(8):
            named = named + (e_iota == ids[k : k + 1, :]).astype(F32)
        before = jnp.dot(
            named.astype(BF16), (e_iota < t_iota).astype(F32).astype(BF16), preferred_element_type=F32
        )
        for k in range(8):
            row = ids[k : k + 1, :]
            position = jnp.sum(jnp.where(e_iota == row, before, 0.0), axis=0, keepdims=True)
            meta[place(0), k : k + 1, 0:64] = row.astype(F32) * 16.0 + position
        meta[place(0), :, 64:128] = wts[...]

    blk[place(0)] = jnp.zeros((64, padded), BF16)
    blk[place(0), :, 0:width] = tok[...]
    for weight in (wg, wu, wd):
        weight[width:padded, :] = jnp.zeros((padded - width, weight.shape[1]), BF16)
    pl.semaphore_wait(barrier, 12)

    def ring_place(way, k):
        return place(k if way == 0 else (NZ - k) % NZ)

    half = 64 // NS
    za, zm = {}, {}
    for way in range(2):
        for k in range(1, 9):
            for sub in range(NS):
                if k == 8 and sub * 2 // NS != way:
                    continue
                rows = pl.ds(sub * half, half)
                src = blk.at[ring_place(way, (k - 1) // 2 * 2), rows]
                za[way, k, sub] = remote(
                    src, blk.at[ring_place(way, k), rows], za_s.at[way, k - 1, sub], za_r.at[way, k - 1, sub],
                    (z_dev if k % 2 else z_two)[way],
                )
            if k < 8 or way == 0:
                zm[way, k] = remote(
                    meta.at[ring_place(way, (k - 1) // 2 * 2)], meta.at[ring_place(way, k)],
                    zm_s.at[way, k - 1], zm_r.at[way, k - 1], (z_dev if k % 2 else z_two)[way],
                )

    def z_go(k):
        for sub in range(NS):
            for way in range(2):
                if k:
                    za[way, k, sub].wait_recv()
                for onward in (k + 2, k + 1):
                    if (way, onward, sub) in za:
                        za[way, onward, sub].start()
        if k == 0:
            routing()
        for way in range(2):
            if k:
                zm[way, k].wait_recv()
            for onward in (k + 2, k + 1):
                if (way, onward) in zm:
                    zm[way, onward].start()

    def z_take(*ks):
        for k in ks:
            for way in range(2):
                for sub in range(NS):
                    if (way, k, sub) in za:
                        za[way, k, sub].wait_recv()
                if (way, k) in zm:
                    zm[way, k].wait_recv()

    lane = lax.broadcasted_iota(jnp.int32, (8, 128), 1)
    row_iota = lax.broadcasted_iota(jnp.int32, (80, 512), 0).astype(F32)
    src_row = (lax.broadcasted_iota(jnp.int32, (1, 512), 1) // 64 * CAP).astype(F32)
    xa = {}
    for g in range(2):
        for j in range(1, NX):
            xa[g, j] = remote(xs.at[g, j - 1], xr.at[g, j], xa_s.at[g, j - 1], xa_r.at[g, j - 1], x_fwd[j])

    def select(g):
        codes, weights = [], []
        for s in range(0, 8, 2):
            a, b = meta[8 * g + s], meta[8 * g + s + 1]
            codes.append(jnp.where(lane < 64, a, pltpu.roll(b, 64, 1)))
            weights.append(jnp.where(lane < 64, pltpu.roll(a, 64, 1), b))
        code = jnp.concatenate(codes, axis=1)
        weight = jnp.concatenate(weights, axis=1)
        rows = blk[8 * g : 8 * g + 8].reshape(512, padded)
        for j in (2, 1, 3, 0):
            base = ((z * NX + (x + j) % NX) * 16).astype(F32)
            own = code - base
            hit = jnp.logical_and(own >= 0.0, own < 16.0)
            slot = jnp.max(jnp.where(hit, own, -1.0), axis=0, keepdims=True)
            share = jnp.sum(jnp.where(hit, weight, 0.0), axis=0, keepdims=True)
            target = jnp.where(slot >= 0.0, slot + src_row, -1.0)
            chosen = row_iota == target
            pick = jnp.dot(chosen.astype(F32).astype(BF16), rows, preferred_element_type=F32).astype(BF16)
            if j:
                xs[g, j - 1] = pick
                xa[g, j].start()
            else:
                xr[g, 0] = pick
            scaled = jnp.where(chosen, share, 0.0)
            high = scaled.astype(BF16)
            wt_hi[g, 80 * j : 80 * j + 80, :] = high
            wt_lo[g, 80 * j : 80 * j + 80, :] = (scaled - high.astype(F32)).astype(BF16)

    def pair(g, s):
        return remote(part.at[g, s, 1 - c], prx.at[g, s], pp_s.at[g, s], pp_r.at[g, s], partner)

    def parts(g, low, high):
        rows = xr[g].reshape(320, padded)

        def piece(s, carry):
            offset = (4 - (s + 1) // 2) * (2 * (s % 2) - 1)
            at = pl.multiple_of((y + NY + offset) % NY * 128, 128)
            gate = jnp.dot(rows, wg[:, pl.ds(at, 128)], preferred_element_type=F32)
            up = jnp.dot(rows, wu[:, pl.ds(at, 128)], preferred_element_type=F32)
            part[g, s, :, 0] = gate.reshape(2, 160, 128)
            part[g, s, :, 1] = up.reshape(2, 160, 128)
            pair(g, s).start()
            return carry

        lax.fori_loop(low, high, piece, 0)

    rs = {}
    for g in range(2):
        for way in range(2):
            for k in range(1, 5):
                for m in range(2):
                    if k == 4 and m != way:
                        continue
                    out_at, in_at = (sb16, rr16) if k > 2 else (sb, rr)
                    rs[g, way, k, m] = remote(
                        out_at.at[g, way, (k - 1) % 2, m], in_at.at[g, way, (k - 1) % 2, m],
                        rs_s.at[g, way, k - 1, m], rs_r.at[g, way, k - 1, m], y_dev[way],
                    )

    def y_step(g, k):
        for s in (0,) if k == 4 else (7 - 2 * k, 8 - 2 * k):
            pair(g, s).wait_recv()
        for m in range(2):
            for way in range(2):
                if (g, way, k, m) not in rs:
                    continue
                s = 0 if k == 4 else 7 - 2 * k + way
                value = part[g, s, c, m] + prx[g, s, m]
                if (g, way, k + 1, m) in rs:
                    rs[g, way, k + 1, m].wait_recv()
                    value = value + (rr16 if k > 1 else rr)[g, way, k % 2, m].astype(F32)
                if k > 2:
                    sb16[g, way, (k - 1) % 2, m] = value.astype(BF16)
                else:
                    sb[g, way, k - 1, m] = value
                rs[g, way, k, m].start()

    def unit(k):
        return (y + 2 * NY - k) % NY

    ag, order = {}, {}
    for g in range(2):
        for way in range(2):
            sign = 1 if way == 0 else -1
            for near in range(1, 5):
                if near == 4 and way != g:
                    continue
                held = hid.at[g, c, unit(0 if near < 3 else 2 * sign)]
                ag[g, sign * near] = remote(
                    held, held, ag_s.at[g, sign * near + 4], ag_r.at[g, sign * near + 4],
                    (y_dev if near % 2 else y_two)[way],
                )
        order[g] = [0, 1, -1, 2, -2, 3, -3, 4 if g == 0 else -4]

    def arrived(g, sigma):
        there = hid.at[g, c, unit(sigma)]
        dev = y_dev[0 if sigma > 0 else 1]
        return remote(there, there, ag_s.at[g, sigma + 4], ag_r.at[g, sigma + 4], dev)

    def hand(g, index, sigma):
        there = hid.at[g, c, unit(sigma)]
        return remote(there, there, ph_s.at[g, index], ph_r.at[g, index], partner)

    def received(g, index, sigma):
        there = hid.at[g, 1 - c, unit(sigma)]
        return remote(there, there, ph_s.at[g, index], ph_r.at[g, index], partner)

    def activate(g):
        pair(g, NY - 1).wait_recv()
        sums = []
        for m in range(2):
            value = part[g, NY - 1, c, m] + prx[g, NY - 1, m]
            for way in range(2):
                rs[g, way, 1, m].wait_recv()
                value = value + rr[g, way, 0, m]
            sums.append(value)
        gate, up = sums
        hid[g, c, unit(0)] = (gate / (1.0 + jnp.exp(-gate)) * up).astype(BF16)
        for sigma in (2, -2, 1, -1):
            ag[g, sigma].start()
        hand(g, 0, 0).start()

    def gather(g, low, high):
        for index in range(low, high):
            sigma = order[g][index]
            arrived(g, sigma).wait_recv()
            if abs(sigma) == 2:
                for onward in (sigma * 2, sigma * 3 // 2):
                    if (g, onward) in ag:
                        ag[g, onward].start()
            hand(g, index, sigma).start()

    xb = {}
    for g in range(2):
        for j in range(1, NX):
            xb[g, j] = remote(ob.at[g, j], yb.at[g, j], xb_s.at[g, j - 1], xb_r.at[g, j - 1], x_bwd[j])

    def down(g):
        for index, sigma in enumerate(order[g]):
            received(g, index, sigma).wait_recv()
        for h in (1, 0):
            rows = jnp.concatenate([hid[g, h, u] for u in range(NY)], axis=1)
            res = lax.dot_general(rows, wd[...], (((1,), (1,)), ((), ())), preferred_element_type=F32)
            res = res.astype(BF16).reshape(2, 80, padded)
            if h:
                ob[g, 2] = res[0]
                xb[g, 2].start()
                ob[g, 3] = res[1]
                xb[g, 3].start()
            else:
                ob[g, 1] = res[1]
                xb[g, 1].start()
                yb[g, 0] = res[0]

    def combine(g):
        for j in range(1, NX):
            xb[g, j].wait_recv()
        rows = yb[g].reshape(320, padded)
        dims = (((0,), (0,)), ((), ()))
        res = lax.dot_general(wt_hi[g], rows, dims, preferred_element_type=F32)
        res = res + lax.dot_general(wt_lo[g], rows, dims, preferred_element_type=F32)
        pt[8 * g : 8 * g + 8] = res.reshape(8, 64, padded)

    low = lax.broadcasted_iota(jnp.int32, (half // 2, 128), 1) < 64

    def pack(to, value):
        for tile in range(3):
            to[tile * half : (tile + 1) * half, :] = value[:, 128 * tile : 128 * tile + 128].astype(BF16)
        rest = value[:, 384:512]
        both = jnp.where(low, rest[: half // 2], pltpu.roll(rest[half // 2 :], 64, 1))
        to[3 * half :, :] = both.astype(BF16)

    def unpack(value):
        value = value.astype(F32)
        both = value[3 * half :]
        rest = jnp.concatenate(
            [jnp.where(low, both, 0.0), jnp.where(low, pltpu.roll(both, 64, 1), 0.0)], axis=0
        )
        return jnp.concatenate([value[tile * half : (tile + 1) * half] for tile in range(3)] + [rest], axis=1)

    zr = {}
    for way in range(2):
        for k in range(1, 9):
            for sub in range(NS):
                if k == 8 and sub * 2 // NS != way:
                    continue
                zr[way, k, sub] = remote(
                    zs.at[way, k - 1, sub], rz.at[way, k - 1, sub], zr_s.at[way, k - 1, sub], zr_r.at[way, k - 1, sub],
                    (z_dev if k % 2 else z_two)[way],
                )

    def z_sum(k):
        for sub in range(NS):
            for way in range(2):
                if (way, k, sub) not in zr:
                    continue
                at = ring_place(1 - way, k)
                value = pt[at, sub * half : (sub + 1) * half, :]
                for before in (k + 1, k + 2):
                    if k % 2 == 0 and (way, before, sub) in zr:
                        zr[way, before, sub].wait_recv()
                        value = value + unpack(rz[way, before - 1, sub])
                pack(zs.at[way, k - 1, sub], value)
                zr[way, k, sub].start()

    def sent(*groups):
        for copies in groups:
            for copy in copies:
                copy.wait_send()

    z_go(0)
    z_go(2)
    z_go(4)
    z_take(1, 3)
    select(0)
    loads[0].wait()
    loads[1].wait()
    for j in range(1, NX):
        xa[0, j].wait_recv()
    parts(0, 0, 1)
    z_go(6)
    y_step(0, 4)
    parts(0, 1, 5)
    z_take(5, 7, 8)
    select(1)
    y_step(0, 3)
    parts(0, 5, 8)
    for j in range(1, NX):
        xa[1, j].wait_recv()
    parts(1, 0, 1)
    y_step(0, 2)
    y_step(1, 4)
    parts(1, 1, 5)
    y_step(0, 1)
    y_step(1, 3)
    parts(1, 5, 8)
    activate(0)
    y_step(1, 2)
    gather(0, 1, 5)
    y_step(1, 1)
    gather(0, 5, 8)
    activate(1)
    loads[2].wait()
    down(0)
    sent(za.values(), zm.values(), xa.values())
    gather(1, 1, 5)
    sent(pair(g, s) for g in range(2) for s in range(NY))
    gather(1, 5, 8)
    down(1)
    combine(0)
    z_sum(3)
    z_sum(1)
    sent(rs.values(), ag.values())
    sent(hand(g, index, sigma) for g in range(2) for index, sigma in enumerate(order[g]))
    combine(1)
    for k in (8, 7, 5, 6, 4, 2):
        z_sum(k)
    sent(xb.values())
    for sub in range(NS):
        total = pt[place(0), sub * half : (sub + 1) * half, :]
        for way in range(2):
            for k in (1, 2):
                zr[way, k, sub].wait_recv()
                total = total + unpack(rz[way, k - 1, sub])
        out[sub * half : (sub + 1) * half, :] = total[:, 0:width].astype(BF16)
    sent(zr.values())


def shards(tokens, expert_ids, combine_weights, w_gate, w_up, w_down):
    rows, width = tokens.shape
    padded = pl.cdiv(width, 128) * 128
    hidden = w_gate.shape[2]
    vmem = pl.BlockSpec(memory_space=pltpu.VMEM)
    hbm = pl.BlockSpec(memory_space=pl.ANY)
    dma = pltpu.SemaphoreType.DMA
    return pl.pallas_call(
        body,
        out_shape=jax.ShapeDtypeStruct((rows, width), BF16),
        in_specs=[vmem, vmem, vmem, hbm, hbm, hbm],
        out_specs=vmem,
        scratch_shapes=[
            pltpu.VMEM((padded, hidden), BF16),
            pltpu.VMEM((padded, hidden), BF16),
            pltpu.VMEM((padded, hidden), BF16),
            pltpu.VMEM((16, 64, padded), BF16),
            pltpu.VMEM((16, 8, 128), F32),
            pltpu.VMEM((2, 3, 80, padded), BF16),
            pltpu.VMEM((2, 4, 80, padded), BF16),
            pltpu.VMEM((2, 320, 512), BF16),
            pltpu.VMEM((2, 320, 512), BF16),
            pltpu.VMEM((2, 8, 2, 2, 160, 128), F32),
            pltpu.VMEM((2, 8, 2, 160, 128), F32),
            pltpu.VMEM((2, 2, 2, 2, 160, 128), F32),
            pltpu.VMEM((2, 2, 2, 2, 160, 128), F32),
            pltpu.VMEM((2, 2, 2, 2, 160, 128), BF16),
            pltpu.VMEM((2, 2, 2, 2, 160, 128), BF16),
            pltpu.VMEM((2, 2, 8, 160, 128), BF16),
            pltpu.VMEM((2, 4, 80, padded), BF16),
            pltpu.VMEM((2, 4, 80, padded), BF16),
            pltpu.VMEM((16, 64, padded), F32),
            pltpu.VMEM((2, 8, NS, 64 // NS * 7 // 2, 128), BF16),
            pltpu.VMEM((2, 8, NS, 64 // NS * 7 // 2, 128), BF16),
            dma((3,)),
            dma((2, 8, NS)),
            dma((2, 8, NS)),
            dma((2, 8)),
            dma((2, 8)),
            dma((2, 3)),
            dma((2, 3)),
            dma((2, 8)),
            dma((2, 8)),
            dma((2, 2, 4, 2)),
            dma((2, 2, 4, 2)),
            dma((2, 9)),
            dma((2, 9)),
            dma((2, 8)),
            dma((2, 8)),
            dma((2, 3)),
            dma((2, 3)),
            dma((2, 8, NS)),
            dma((2, 8, NS)),
        ],
        compiler_params=pltpu.CompilerParams(
            collective_id=0, has_side_effects=True, vmem_limit_bytes=60 * 1024 * 1024
        ),
    )(tokens, expert_ids.T, combine_weights.T, w_gate, w_up, w_down.transpose(0, 2, 1))


def solution(mesh):
    placed = (
        P("expert", "dp"),
        P("expert", None),
        P("expert", None),
        P("expert", "dp", None),
        P("expert", "dp", None),
        P("expert", None, "dp"),
    )
    return jax.shard_map(
        shards, mesh=mesh, in_specs=placed, out_specs=P("expert", "dp"), check_vma=False
    )
```
